32 devices in a mesh: lat: 8 (over z, y), lon: 4 (over x, core).
Axes of the slice: x: 2, y: 2, z: 4, core: 2. Of those that a mesh axis runs over, the one named last changes fastest.
Arguments:
- grid_field: float32 [384, 64, 512], P(None, 'lat', 'lon'), may hold values from -6 to 6
- disco_dlat: int32 [64, 16], P('lat'), may hold values from -2 to 2
- disco_dlon: int32 [64, 16], P('lat'), may hold values from -2 to 2
- disco_basis: int32 [64, 16], P('lat'), may hold values from 0 to 3
- disco_quad: float32 [64, 16], P('lat'), may hold values from 0.05 to 0.5
- disco_weight: bfloat16 [4, 384, 384], replicated, may hold values from -0.3125 to 0.3125
- norm_gain: float32 [384], replicated, may hold values from 0.1 to 1.9
- spectral_filter: float32 [384, 64], replicated, may hold values from -6 to 6
- mix_weight: bfloat16 [384, 384], replicated, may hold values from -0.3125 to 0.3125
Outputs:
- updated: float32 [384, 64, 512], P(None, 'lat', 'lon')
The draws below stay inside these ranges and needn't reach their ends.
All inputs are finite; a program needn't handle non-finite values.
Results may differ from the reference program's by a relative error of at most 0.0044.
Values may be sent and summed in bfloat16 or wider, within the bound.
A program may use at most 64 MiB of HBM per device.

```python
import math
import jax
import jax.numpy as jnp
from jax import lax

C = 384
HALO = 2
KSUP = 16
NBASIS = 4
NLAT = 64
NLON = 512
MM = 64
LL = 64


def plant(result, stream_key, least, top_value):
    place = [jax.random.randint(jax.random.fold_in(stream_key, axis), (), 0, length) for axis, length in enumerate(result.shape)]
    widest = result.shape.index(max(result.shape))
    beside = place[:widest] + [(place[widest] + 1) % result.shape[widest]] + place[widest + 1:]
    return result.at[tuple(place)].set(least).at[tuple(beside)].set(top_value)


def block_levels(stream_key, extent, split, least, largest):
    def one(position, blocks):
        steps = jax.random.uniform(jax.random.fold_in(jax.random.fold_in(stream_key, 6), position), (blocks,), jnp.float32, least / len(split), largest / len(split))
        return jnp.repeat(jnp.exp(steps), extent[position] // blocks).reshape((-1,) + (1,) * (len(extent) - position - 1))

    gain = one(*split[0])
    for cut in split[1:]:
        gain = gain * one(*cut)
    return gain


def centred(stream_key, dims, deviation, reach, shards=(), kind=jnp.bfloat16):
    array = deviation * jax.random.normal(stream_key, dims, jnp.float32)
    if shards:
        array = array * block_levels(stream_key, dims, shards, -0.22, 0.18)
    return jnp.clip(array, -reach, reach).astype(kind)


def setup_inputs(seed: int = 0) -> dict:
    key_of = jax.random.split(jax.random.key(seed), 10)
    return {
        "grid_field": centred(key_of[0], (C, NLAT, NLON), 1.0, 6.0, ((1, 8), (2, 4)), jnp.float32),
        "disco_dlat": plant(jax.random.randint(key_of[1], (NLAT, KSUP), -HALO, HALO + 1), jax.random.fold_in(key_of[1], 1), -HALO, HALO).astype(jnp.int32),
        "disco_dlon": plant(jax.random.randint(key_of[2], (NLAT, KSUP), -HALO, HALO + 1), jax.random.fold_in(key_of[2], 1), -HALO, HALO).astype(jnp.int32),
        "disco_basis": plant(jax.random.randint(key_of[3], (NLAT, KSUP), 0, NBASIS), jax.random.fold_in(key_of[3], 1), 0, NBASIS - 1).astype(jnp.int32),
        "disco_quad": jnp.clip(jnp.exp(math.log(0.5) - 2.3025851 * jax.random.uniform(key_of[4], (NLAT, KSUP), jnp.float32) ** block_levels(key_of[4], (NLAT, KSUP), ((0, 8),), -0.2, 0.2)), 0.05, 0.5),
        "disco_weight": centred(key_of[5], (NBASIS, C, C), C ** -0.5, 0.3125),
        "norm_gain": jnp.clip(1.0 + 0.18 * jax.random.normal(key_of[6], (C,), jnp.float32), 0.1, 1.9),
        "spectral_filter": centred(key_of[7], (C, LL), 1.0, 6.0, (), jnp.float32),
        "mix_weight": centred(key_of[8], (C, C), C ** -0.5, 0.3125),
    }


def legendre_table(first_order, local_orders, all_orders, degrees, nlat):
    lat_pos = jnp.arange(nlat, dtype=jnp.float32)
    colatitude = math.pi * (lat_pos + 0.5) / nlat
    cosine = jnp.cos(colatitude)
    sine = jnp.sin(colatitude)
    counters = jnp.arange(1, all_orders, dtype=jnp.float32)
    cumulative = jnp.concatenate([jnp.zeros((1,), jnp.float32), jnp.cumsum(jnp.log((2.0 * counters - 1.0) / (2.0 * counters)))])
    log_product = lax.dynamic_slice_in_dim(cumulative, first_order, local_orders)
    orders = first_order + jnp.arange(local_orders, dtype=jnp.int32)
    order_real = orders.astype(jnp.float32)[:, None]
    log_seed = 0.5 * (jnp.log((2.0 * order_real + 1.0) / (4.0 * math.pi)) + log_product[:, None]) + order_real * jnp.log(sine)[None, :]
    rescale = jnp.clip(-log_seed, 0.0, 80.0)
    seed_value = jnp.exp(log_seed + rescale)
    undo = jnp.exp(-rescale)

    def advance(state_pair, degree):
        previous, before_last = state_pair
        degree_real = degree.astype(jnp.float32)
        factor_a = jnp.sqrt(jnp.maximum(4.0 * degree_real ** 2 - 1.0, 1.0) / jnp.maximum(degree_real ** 2 - order_real ** 2, 1.0))
        factor_b = jnp.sqrt(jnp.maximum((degree_real - 1.0) ** 2 - order_real ** 2, 0.0) / jnp.maximum(4.0 * (degree_real - 1.0) ** 2 - 1.0, 1.0))
        recurred = factor_a * (cosine[None, :] * previous - factor_b * before_last)
        current = jnp.where(degree == orders[:, None], seed_value, jnp.where(degree > orders[:, None], recurred, 0.0))
        return ((current, previous), current * undo)
    empty = jnp.zeros((local_orders, nlat), jnp.float32)
    final_pair, table = lax.scan(advance, (empty, empty), jnp.arange(degrees, dtype=jnp.int32), unroll=8)
    return table

def disco_rows(padded, disco_dlat, disco_dlon, disco_basis, disco_quad, disco_weight, width):
    basis_count = disco_weight.shape[0]
    channels = padded.shape[0]
    zero_index = jnp.zeros((), jnp.int32)

    def one_row(inputs):
        row_index, lat_offsets, lon_offsets, basis_row, quad_row = inputs
        sources = (row_index + HALO + lat_offsets).astype(jnp.int32)
        begins = (HALO + lon_offsets).astype(jnp.int32)

        def take(source, begin):
            return lax.dynamic_slice(padded, (zero_index, source, begin), (channels, 1, width))[:, 0, :]
        support = jax.vmap(take)(sources, begins)
        selector = (basis_row[:, None] == jnp.arange(basis_count, dtype=jnp.int32)[None, :]).astype(jnp.float32) * quad_row[:, None]
        aggregate = jnp.einsum('kb,kcj->bcj', selector, support, precision=lax.Precision.HIGHEST).astype(jnp.bfloat16)
        return lax.dot_general(disco_weight, aggregate, (((0, 1), (0, 1)), ((), ())), preferred_element_type=jnp.float32)
    row_count = disco_dlat.shape[0]
    stacked = lax.map(one_row, (jnp.arange(row_count, dtype=jnp.int32), disco_dlat, disco_dlon, disco_basis, disco_quad))
    return jnp.transpose(stacked, (1, 0, 2))

def reference(grid_field, disco_dlat, disco_dlon, disco_basis, disco_quad, disco_weight, norm_gain, spectral_filter, mix_weight):
    padded = jnp.pad(grid_field, ((0, 0), (HALO, HALO), (0, 0)))
    padded = jnp.concatenate([padded[:, :, NLON - HALO:], padded, padded[:, :, :HALO]], axis=2)
    after_conv = grid_field + disco_rows(padded, disco_dlat, disco_dlon, disco_basis, disco_quad, disco_weight, NLON)
    mean_square = lax.optimization_barrier(jnp.mean(after_conv * after_conv, axis=0, keepdims=True))
    normed = after_conv * lax.rsqrt(mean_square + 1e-06) * norm_gain[:, None, None]
    spectrum = jnp.fft.rfft(normed, axis=2)[:, :, :MM] * (2.0 * math.pi / NLON)
    fourier = jnp.stack([jnp.real(spectrum), jnp.imag(spectrum)]).astype(jnp.float32)
    lat_pos = jnp.arange(NLAT, dtype=jnp.float32)
    quad_weight = math.pi / NLAT * jnp.sin(math.pi * (lat_pos + 0.5) / NLAT)
    weighted = jnp.transpose(fourier, (3, 0, 1, 2)) * quad_weight
    table = legendre_table(0, MM, MM, LL, NLAT)

    def per_order(inputs):
        portion, order_table = inputs
        spectra = jnp.einsum('rck,lk->rcl', portion, order_table, precision=lax.Precision.HIGHEST)
        filtered = spectra * spectral_filter[None]
        return jnp.einsum('rcl,lk->rck', filtered, order_table, precision=lax.Precision.HIGHEST)
    synthesis = lax.map(per_order, (weighted, jnp.transpose(table, (1, 0, 2))))
    complex_part = lax.complex(synthesis[:, 0], synthesis[:, 1])
    complex_part = jnp.transpose(complex_part, (1, 2, 0))
    complex_part = jnp.pad(complex_part, ((0, 0), (0, 0), (0, NLON // 2 + 1 - MM)))
    wave_field = (jnp.fft.irfft(complex_part, n=NLON, axis=2) * NLON).astype(jnp.float32)
    activated = jax.nn.gelu(wave_field, approximate=True).astype(jnp.bfloat16)
    mixed = jnp.dot(jnp.transpose(mix_weight), activated.reshape(C, NLAT * NLON), preferred_element_type=jnp.float32)
    return after_conv + mixed.reshape(C, NLAT, NLON)
```

```python
import functools
import math

import jax
import jax.numpy as jnp
import numpy as np
from jax import lax
from jax.experimental import pallas as pl
from jax.experimental.pallas import tpu as pltpu
from jax.sharding import PartitionSpec as P

M_DEV = 8
HALO = 2
PAD = 16
LANES = 128
MESH = pl.DeviceIdType.MESH
VM = pl.BlockSpec(memory_space=pltpu.VMEM)
SM = pl.BlockSpec(memory_space=pltpu.SMEM)


def halo_kernel(lat_n, lon_n, x_ref, xp_ref, xt_ref, send_sem, recv_sem):
    rows, width, chans = xt_ref.shape
    lat, lon = lax.axis_index("lat"), lax.axis_index("lon")
    up, down = lax.rem(lat + lat_n - 1, lat_n), lax.rem(lat + 1, lat_n)
    left, right = lax.rem(lon + lon_n - 1, lon_n), lax.rem(lon + 1, lon_n)
    barrier = pltpu.get_barrier_semaphore()
    peers = [(a, b) for a in (up, lat, down) for b in (left, lon, right)]
    peers.pop(4)
    for peer in peers:
        pl.semaphore_signal(barrier, inc=1, device_id=peer, device_id_type=MESH)

    def turn(row):
        cells = x_ref[:, row, :].T
        xt_ref[row] = cells
        xp_ref[row + HALO, PAD : PAD + width, :] = cells.astype(jnp.bfloat16)

    edge = list(range(HALO)) + list(range(rows - HALO, rows))
    for row in edge:
        turn(row)
    pl.semaphore_wait(barrier, len(peers))
    row_spans = {
        -1: (HALO, rows + HALO, HALO),
        0: (HALO, HALO, rows),
        1: (rows, 0, HALO),
    }
    col_spans = {
        -1: (PAD, PAD + width, PAD),
        0: (PAD, PAD, width),
        1: (width, 0, PAD),
    }
    copies = []

    def send(dv, dh):
        peer = ({-1: up, 0: lat, 1: down}[dv], {-1: left, 0: lon, 1: right}[dh])
        rs, rd, rn = row_spans[dv]
        cs, cd, cn = col_spans[dh]
        index = (dv + 1) * 3 + dh + 1
        copy = pltpu.make_async_remote_copy(
            src_ref=xp_ref.at[rs : rs + rn, cs : cs + cn, :],
            dst_ref=xp_ref.at[rd : rd + rn, cd : cd + cn, :],
            send_sem=send_sem.at[index],
            recv_sem=recv_sem.at[index],
            device_id=peer,
            device_id_type=MESH,
        )
        copy.start()
        copies.append(copy)

    for dv in (-1, 1):
        for dh in (0, -1, 1):
            send(dv, dh)
    for row in range(HALO, rows - HALO):
        turn(row)
    for dh in (-1, 1):
        send(0, dh)
    for copy in copies:
        copy.wait()


def conv_kernel(
    src_ref, begin_ref, basis_ref, quad_ref, xp_ref, xt_ref, w_ref, gain_ref, table_ref,
    ac_ref, fp_ref, y_ref,
):
    rows, width, chans = xt_ref.shape
    basis_count = w_ref.shape[0]
    taps = src_ref.shape[1]
    slabs = chans // LANES
    tall = xp_ref.shape[1]

    @pl.loop(0, rows + 2 * HALO)
    def _(row):
        cells = xp_ref[row]
        for b in range(basis_count):
            mixed = jnp.dot(cells, w_ref[b], preferred_element_type=jnp.float32)
            for c in range(slabs):
                y_ref[b // 2, row, c, pl.ds(b % 2, tall, stride=2), :] = mixed[
                    :, c * LANES : (c + 1) * LANES
                ]

    step = 32

    @pl.loop(0, rows)
    def _(row):
        @pl.loop(0, width // step)
        def _(part):
            base = pl.multiple_of(part * step, step)
            totals = [
                xt_ref[row, pl.ds(base, step), c * LANES : (c + 1) * LANES] for c in range(slabs)
            ]
            for k in range(taps):
                basis, source, scale = basis_ref[row, k], src_ref[row, k], quad_ref[row, k]
                begin = 2 * (base + begin_ref[row, k]) + (basis & 1)
                for c in range(slabs):
                    totals[c] = totals[c] + scale * y_ref[
                        basis >> 1, source, c, pl.ds(begin, step, stride=2), :
                    ]
            for c in range(slabs):
                ac_ref[row, pl.ds(base, step), c * LANES : (c + 1) * LANES] = totals[c]

        cells = ac_ref[row]
        mean = jnp.mean(cells * cells, axis=1, keepdims=True)
        normed = cells * lax.rsqrt(mean + 1e-06) * gain_ref[...]
        fp_ref[row] = jnp.dot(
            table_ref[...], normed.astype(jnp.bfloat16), preferred_element_type=jnp.float32
        ).astype(jnp.bfloat16)


def spectral_kernel(
    lat_n, lon_n, fp_ref, ac_ref, ab_ref, seed_ref, undo_ref, quadw_ref, filt_ref,
    out_ref,
    recv1, red, snd2, recv2, legendre, back, snd3,
    s1, r1, s2, r2, s3, r3, s4, r4,
):
    rows, all_q, chans = fp_ref.shape
    group = all_q // lon_n
    count = group // lat_n
    degrees, _, nlat = ac_ref.shape
    wire = snd2.dtype
    lat, lon = lax.axis_index("lat"), lax.axis_index("lon")

    barrier = pltpu.get_barrier_semaphore()
    for off in range(1, lon_n):
        pl.semaphore_signal(
            barrier, inc=1, device_id=(lat, lax.rem(lon + off, lon_n)), device_id_type=MESH
        )
    for off in range(1, lat_n):
        pl.semaphore_signal(
            barrier, inc=1, device_id=(lax.rem(lat + off, lat_n), lon), device_id_type=MESH
        )
    pl.semaphore_wait(barrier, lon_n + lat_n - 2)

    first = []
    for off in range(1, lon_n):
        peer = lax.rem(lon + off, lon_n)
        copy = pltpu.make_async_remote_copy(
            src_ref=fp_ref.at[:, pl.ds(pl.multiple_of(peer * group, group), group), :],
            dst_ref=recv1.at[off - 1],
            send_sem=s1.at[off - 1],
            recv_sem=r1.at[off - 1],
            device_id=(lat, peer),
            device_id_type=MESH,
        )
        copy.start()
        first.append(copy)

    zero = undo_ref[...] * 0.0

    def advance(degree, pair):
        previous, older = pair
        current = ac_ref[degree] * previous - ab_ref[degree] * older + seed_ref[degree]
        legendre[degree] = current * undo_ref[...]
        return (current, previous)

    lax.fori_loop(0, degrees, advance, (zero, zero), unroll=4)

    for copy in first:
        copy.wait()
    mine = pl.ds(pl.multiple_of(lon * group, group), group)
    for row in range(rows):
        total = fp_ref[row, mine, :].astype(jnp.float32)
        for off in range(1, lon_n):
            total = total + recv1[off - 1, row].astype(jnp.float32)
        red[:, row, :] = total
    for d in range(lat_n):
        snd2[d] = red[d * count : (d + 1) * count].reshape(count * rows, chans).astype(wire)

    second = []
    for off in range(1, lat_n):
        peer = lax.rem(lat + off, lat_n)
        copy = pltpu.make_async_remote_copy(
            src_ref=snd2.at[peer],
            dst_ref=recv2.at[lat],
            send_sem=s2.at[off - 1],
            recv_sem=r2.at[off - 1],
            device_id=(peer, lon),
            device_id_type=MESH,
        )
        copy.start()
        second.append(copy)
    recv2[lat] = snd2[lat]
    tables = [legendre[:, t, :] for t in range(count)]
    for copy in second:
        copy.wait()

    for t in range(count):
        cells = recv2[:, t * rows : (t + 1) * rows, :].astype(jnp.float32)
        cells = cells.reshape(lat_n * rows, chans).astype(jnp.bfloat16)
        analysis = (tables[t] * quadw_ref[...]).astype(jnp.bfloat16)
        spectra = jnp.dot(analysis, cells, preferred_element_type=jnp.float32)
        filtered = (spectra * filt_ref[...]).astype(jnp.bfloat16)
        result = jnp.dot(
            tables[t].T.astype(jnp.bfloat16), filtered, preferred_element_type=jnp.float32
        )
        back[:, t * rows : (t + 1) * rows, :] = result.reshape(lat_n, rows, chans)
    for d in range(lat_n):
        snd3[d] = back[d].astype(wire)

    third = []
    for off in range(1, lat_n):
        peer = lax.rem(lat + off, lat_n)
        copy = pltpu.make_async_remote_copy(
            src_ref=snd3.at[peer],
            dst_ref=out_ref.at[lon, lat],
            send_sem=s3.at[off - 1],
            recv_sem=r3.at[off - 1],
            device_id=(peer, lon),
            device_id_type=MESH,
        )
        copy.start()
        third.append(copy)
    out_ref[lon, lat] = snd3[lat]

    fourth = []

    def spread(source, slot):
        for off in range(1, lon_n):
            peer = lax.rem(lon + off, lon_n)
            copy = pltpu.make_async_remote_copy(
                src_ref=out_ref.at[lon, source],
                dst_ref=out_ref.at[lon, source],
                send_sem=s4.at[slot, off - 1],
                recv_sem=r4.at[slot, off - 1],
                device_id=(lat, peer),
                device_id_type=MESH,
            )
            copy.start()
            fourth.append(copy)

    spread(lat, 0)
    for off in range(1, lat_n):
        third[off - 1].wait()
        spread(lax.rem(lat + lat_n - off, lat_n), off)
    for copy in fourth:
        copy.wait()


def output_kernel(syn_ref, ac_ref, table_ref, mix_ref, o_ref, wide):
    rows, width, chans = ac_ref.shape
    all_q = table_ref.shape[1]
    wide[...] = syn_ref[...].astype(jnp.float32).reshape(all_q, rows, chans)
    for row in range(rows):
        waves = wide[:, row, :].astype(jnp.bfloat16)
        field = jnp.dot(table_ref[...], waves, preferred_element_type=jnp.float32)
        active = jax.nn.gelu(field, approximate=True).astype(jnp.bfloat16)
        total = ac_ref[row] + jnp.dot(active, mix_ref[...], preferred_element_type=jnp.float32)
        o_ref[:, row, :] = total.T


def per_device(
    grid_field,
    disco_dlat,
    disco_dlon,
    disco_basis,
    disco_quad,
    disco_weight,
    norm_gain,
    spectral_filter,
    mix_weight,
):
    lat_n = lax.axis_size("lat")
    lon_n = lax.axis_size("lon")
    chans, rows, width = grid_field.shape
    nlat, nlon = rows * lat_n, width * lon_n
    modes = M_DEV * lat_n
    all_q = 2 * modes
    degrees = spectral_filter.shape[1]
    group = all_q // lon_n
    count = group // lat_n
    basis_count = disco_weight.shape[0]
    lat, lon = lax.axis_index("lat"), lax.axis_index("lon")
    f32, bf16 = jnp.float32, jnp.bfloat16

    xp, xt = pl.pallas_call(
        functools.partial(halo_kernel, lat_n, lon_n),
        out_shape=(
            jax.ShapeDtypeStruct((rows + 2 * HALO, width + 2 * PAD, chans), bf16),
            jax.ShapeDtypeStruct((rows, width, chans), f32),
        ),
        in_specs=[VM],
        out_specs=(VM, VM),
        scratch_shapes=[pltpu.SemaphoreType.DMA((9,)), pltpu.SemaphoreType.DMA((9,))],
        compiler_params=pltpu.CompilerParams(collective_id=0, has_side_effects=True),
    )(grid_field)

    q_pos = jnp.arange(all_q, dtype=jnp.int32)
    j_pos = lon * width + jnp.arange(width, dtype=jnp.int32)
    turns = (j_pos[:, None] * (q_pos // 2)[None, :] + (q_pos % 2)[None, :] * (nlon // 4)) % nlon
    wave = jnp.cos(turns.astype(f32) * (2.0 * math.pi / nlon))
    forward = (wave.T * (2.0 * math.pi / nlon)).astype(bf16)
    inverse = (wave * jnp.where(q_pos < 2, 1.0, 2.0)[None, :]).astype(bf16)

    row_pos = jnp.arange(rows, dtype=jnp.int32)[:, None]
    source = row_pos + disco_dlat
    globally = lat * rows + source
    quad = jnp.where((globally >= 0) & (globally < nlat), disco_quad, 0.0)

    after_conv, partial = pl.pallas_call(
        conv_kernel,
        out_shape=(
            jax.ShapeDtypeStruct((rows, width, chans), f32),
            jax.ShapeDtypeStruct((rows, all_q, chans), bf16),
        ),
        in_specs=[SM] * 4 + [VM] * 5,
        out_specs=(VM, VM),
        scratch_shapes=[
            pltpu.VMEM(
                (
                    (basis_count + 1) // 2,
                    rows + 2 * HALO,
                    chans // LANES,
                    2 * (width + 2 * PAD),
                    LANES,
                ),
                f32,
            )
        ],
    )(
        source + HALO, disco_dlon + PAD, disco_basis, quad,
        xp, xt, disco_weight, norm_gain[None, :], forward,
    )

    lat_pos = jnp.arange(nlat, dtype=f32)
    colatitude = math.pi * (lat_pos + 0.5) / nlat
    cosine, sine = jnp.cos(colatitude), jnp.sin(colatitude)
    order = ((lon * group + lat * count + jnp.arange(count, dtype=jnp.int32)) // 2).astype(f32)
    counters = jnp.arange(1, modes, dtype=f32)
    logs = jnp.log((2.0 * counters - 1.0) / (2.0 * counters))
    log_product = jnp.sum(jnp.where(counters[None, :] <= order[:, None], logs[None, :], 0.0), 1)
    om = order[:, None]
    log_seed = (
        0.5 * (jnp.log((2.0 * om + 1.0) / (4.0 * math.pi)) + log_product[:, None])
        + om * jnp.log(sine)[None, :]
    )
    rescale = jnp.clip(-log_seed, 0.0, 80.0)
    seed_value = jnp.exp(log_seed + rescale)
    undo = jnp.exp(-rescale)
    ell = jnp.arange(degrees, dtype=f32)[:, None, None]
    om3 = order[None, :, None]
    a = jnp.sqrt(jnp.maximum(4.0 * ell**2 - 1.0, 1.0) / jnp.maximum(ell**2 - om3**2, 1.0))
    b = jnp.sqrt(
        jnp.maximum((ell - 1.0) ** 2 - om3**2, 0.0)
        / jnp.maximum(4.0 * (ell - 1.0) ** 2 - 1.0, 1.0)
    )
    a = jnp.where(ell > om3, a, 0.0)
    a_cos = a * cosine[None, None, :]
    a_b = jnp.broadcast_to(a * b, a_cos.shape)
    seeds = jnp.where(ell == om3, seed_value[None], 0.0)
    quad_weight = (math.pi / nlat * sine)[None, :]

    wire = bf16 if (count * rows) % 16 == 0 else f32
    block = (lat_n, count * rows, chans)
    dma = pltpu.SemaphoreType.DMA
    synthesis = pl.pallas_call(
        functools.partial(spectral_kernel, lat_n, lon_n),
        out_shape=jax.ShapeDtypeStruct((lon_n,) + block, wire),
        in_specs=[VM] * 7,
        out_specs=VM,
        scratch_shapes=[
            pltpu.VMEM((lon_n - 1, rows, group, chans), bf16),
            pltpu.VMEM((group, rows, chans), f32),
            pltpu.VMEM(block, wire),
            pltpu.VMEM(block, wire),
            pltpu.VMEM((degrees, count, nlat), f32),
            pltpu.VMEM(block, f32),
            pltpu.VMEM(block, wire),
            dma((lon_n - 1,)), dma((lon_n - 1,)),
            dma((lat_n - 1,)), dma((lat_n - 1,)),
            dma((lat_n - 1,)), dma((lat_n - 1,)),
            dma((lat_n, lon_n - 1)), dma((lat_n, lon_n - 1)),
        ],
        compiler_params=pltpu.CompilerParams(collective_id=1, has_side_effects=True),
    )(partial, a_cos, a_b, seeds, undo, quad_weight, spectral_filter.T)

    return pl.pallas_call(
        output_kernel,
        out_shape=jax.ShapeDtypeStruct((chans, rows, width), f32),
        in_specs=[VM] * 4,
        out_specs=VM,
        scratch_shapes=[pltpu.VMEM((all_q, rows, chans), f32)],
    )(synthesis, after_conv, inverse, mix_weight)


def solution(mesh):
    placed = (
        P(None, "lat", "lon"),
        P("lat", None),
        P("lat", None),
        P("lat", None),
        P("lat", None),
        P(),
        P(),
        P(),
        P(),
    )
    return jax.shard_map(
        per_device, mesh=mesh, in_specs=placed, out_specs=P(None, "lat", "lon"), check_vma=False
    )
```

```python
import functools
import math

import jax
import jax.numpy as jnp
from jax import lax
from jax.experimental import pallas as pl
from jax.experimental.pallas import tpu as pltpu
from jax.sharding import PartitionSpec as P

M_DEV = 8
HALO = 2
PAD = 16
LANES = 128
MESH = pl.DeviceIdType.MESH
VM = pl.BlockSpec(memory_space=pltpu.VMEM)
SM = pl.BlockSpec(memory_space=pltpu.SMEM)


def order_tables(forward_ref, inverse_ref, lon, nlon):
    width, all_q = inverse_ref.shape

    def wave(shape, q_axis):
        q = lax.broadcasted_iota(jnp.int32, shape, q_axis)
        j = lax.broadcasted_iota(jnp.int32, shape, 1 - q_axis) + lon * width
        turns = (j * (q >> 1) + (q & 1) * (nlon // 4)).astype(jnp.float32)
        turns = turns - nlon * jnp.floor(turns * (1.0 / nlon))
        return q, jnp.cos(turns * (2.0 * math.pi / nlon))

    q, cells = wave((all_q, width), 0)
    forward_ref[...] = (cells * (2.0 * math.pi / nlon)).astype(forward_ref.dtype)
    q, cells = wave((width, all_q), 1)
    inverse_ref[...] = (cells * jnp.where(q < 2, 1.0, 2.0)).astype(inverse_ref.dtype)


def legendre_table(table_ref, start_ref, first_q, modes):
    degrees, count, nlat = table_ref.shape
    shape = (count, nlat)

    def order_of(dims):
        q = lax.broadcasted_iota(jnp.int32, dims, 0) + first_q
        return (q >> 1).astype(jnp.float32)

    order = order_of(shape)
    colatitude = (
        (lax.broadcasted_iota(jnp.int32, shape, 1).astype(jnp.float32) + 0.5) * math.pi / nlat
    )
    cosine, sine = jnp.cos(colatitude), jnp.sin(colatitude)
    counters = lax.broadcasted_iota(jnp.int32, (count, modes), 1).astype(jnp.float32) + 1.0
    logs = jnp.log((2.0 * counters - 1.0) / (2.0 * counters))
    logs = jnp.where(counters <= order_of((count, modes)), logs, 0.0)
    log_product = jnp.sum(logs, axis=1, keepdims=True)
    log_seed = 0.5 * (
        jnp.log((2.0 * order + 1.0) / (4.0 * math.pi)) + log_product
    ) + order * jnp.log(sine)
    rescale = jnp.clip(-log_seed, 0.0, 80.0)
    seed = jnp.exp(log_seed + rescale)
    undo = jnp.exp(-rescale)
    square = order * order
    start_ref[...] = jnp.zeros(start_ref.shape, jnp.float32)

    def advance(degree, pair):
        previous, older = pair
        ell = degree.astype(jnp.float32)
        a = jnp.sqrt(
            jnp.maximum(4.0 * ell * ell - 1.0, 1.0) / jnp.maximum(ell * ell - square, 1.0)
        )
        below = (ell - 1.0) * (ell - 1.0)
        b = jnp.sqrt(jnp.maximum(below - square, 0.0) / jnp.maximum(4.0 * below - 1.0, 1.0))
        current = jnp.where(
            order == ell, seed, jnp.where(ell > order, a * (cosine * previous - b * older), 0.0)
        )
        table_ref[degree] = current * undo
        return (current, previous)

    lax.fori_loop(0, degrees, advance, (start_ref[0], start_ref[1]), unroll=4)


def field_kernel(
    lat_n, lon_n, modes,
    dlat_ref, dlon_ref, basis_ref, quad_ref, x_ref, w_ref, gain_ref, filt_ref,
    out_ref, ac_ref, inverse_ref,
    xp_ref, y_ref, forward, fp_ref, recv_a, send_b, recv_b, red, snd2, recv2,
    legendre, start, back, snd3,
    halo_s, halo_r, sa, ra, sb, rb, s2, r2, s3, r3, sx, rx, sp, rp, sf, rf,
):
    rows, width, chans = ac_ref.shape
    basis_count = w_ref.shape[0]
    taps = dlat_ref.shape[1]
    slabs = chans // LANES
    tall = xp_ref.shape[1]
    all_q = forward.shape[0]
    half = all_q // 2
    chips = lon_n // 2
    group = all_q // lon_n
    count = group // lat_n
    nlat, nlon = lat_n * rows, lon_n * width
    wire = snd2.dtype
    lat, lon = lax.axis_index("lat"), lax.axis_index("lon")
    up, down = lax.rem(lat + lat_n - 1, lat_n), lax.rem(lat + 1, lat_n)
    left, right = lax.rem(lon + lon_n - 1, lon_n), lax.rem(lon + 1, lon_n)
    chip, core = lon // 2, lax.rem(lon, 2)
    mate = chip * 2 + 1 - core

    def remote(source, target, send, recv, peer):
        return pltpu.make_async_remote_copy(
            src_ref=source, dst_ref=target, send_sem=send, recv_sem=recv,
            device_id=peer, device_id_type=MESH,
        )

    barrier = pltpu.get_barrier_semaphore()
    peers = [(lax.rem(lat + off, lat_n), lon) for off in range(1, lat_n)]
    peers += [(lat, lax.rem(lon + off, lon_n)) for off in range(1, lon_n)]
    peers += [(a, b) for a in (up, down) for b in (left, right)]
    for peer in peers:
        pl.semaphore_signal(barrier, inc=1, device_id=peer, device_id_type=MESH)

    def turn(row):
        cells = x_ref[:, row, :].T
        ac_ref[row] = cells
        xp_ref[row + HALO, PAD : PAD + width, :] = cells.astype(jnp.bfloat16)

    row_spans = {-1: (HALO, rows + HALO, HALO), 0: (HALO, HALO, rows), 1: (rows, 0, HALO)}
    col_spans = {-1: (PAD, PAD + width, PAD), 0: (PAD, PAD, width), 1: (width, 0, PAD)}

    def halo(dv, dh):
        peer = ({-1: up, 0: lat, 1: down}[dv], {-1: left, 0: lon, 1: right}[dh])
        rs, rd, rn = row_spans[dv]
        cs, cd, cn = col_spans[dh]
        index = (dv + 1) * 3 + dh + 1
        return remote(
            xp_ref.at[rs : rs + rn, cs : cs + cn, :],
            xp_ref.at[rd : rd + rn, cd : cd + cn, :],
            halo_s.at[index], halo_r.at[index], peer,
        )

    for row in list(range(HALO)) + list(range(rows - HALO, rows)):
        turn(row)
    pl.semaphore_wait(barrier, len(peers))
    across = [halo(dv, dh) for dv in (-1, 1) for dh in (0, -1, 1)]
    for copy in across:
        copy.start()
    for row in range(HALO, rows - HALO):
        turn(row)
    beside = [halo(0, dh) for dh in (-1, 1)]
    for copy in beside:
        copy.start()

    order_tables(forward, inverse_ref, lon, nlon)
    place = core * chips + chip
    legendre_table(legendre, start, place * group + lat * count, modes)
    for copy in beside:
        copy.wait()

    def mix(row):
        cells = xp_ref[row]
        for b in range(basis_count):
            mixed = jnp.dot(cells, w_ref[b], preferred_element_type=jnp.float32)
            for c in range(slabs):
                y_ref[b // 2, row, c, pl.ds(b % 2, tall, stride=2), :] = mixed[
                    :, c * LANES : (c + 1) * LANES
                ]

    step = 32

    def to_mate(row):
        return remote(
            fp_ref.at[row, 1 - core], recv_a.at[row], sa.at[row], ra.at[row], (lat, mate)
        )

    def to_chip(row, off):
        peer = lax.rem(chip + off, chips)
        return remote(
            send_b.at[row, peer], recv_b.at[off - 1, row],
            sb.at[row, off - 1], rb.at[row, off - 1], (lat, peer * 2 + core),
        )

    def conv(row):
        @pl.loop(0, width // step)
        def _(part):
            base = pl.multiple_of(part * step, step)
            totals = [
                ac_ref[row, pl.ds(base, step), c * LANES : (c + 1) * LANES] for c in range(slabs)
            ]
            for k in range(taps):
                basis = basis_ref[row, k]
                source = row + dlat_ref[row, k]
                globally = source + lat * rows
                inside = jnp.logical_and(globally >= 0, globally < nlat)
                scale = jnp.where(inside, quad_ref[row, k], 0.0)
                begin = 2 * (base + dlon_ref[row, k] + PAD) + (basis & 1)
                for c in range(slabs):
                    totals[c] = totals[c] + scale * y_ref[
                        basis >> 1, source + HALO, c, pl.ds(begin, step, stride=2), :
                    ]
            for c in range(slabs):
                ac_ref[row, pl.ds(base, step), c * LANES : (c + 1) * LANES] = totals[c]

        cells = ac_ref[row]
        mean = jnp.mean(cells * cells, axis=1, keepdims=True)
        normed = cells * lax.rsqrt(mean + 1e-06) * gain_ref[...]
        fp_ref[row] = jnp.dot(
            forward[...], normed.astype(jnp.bfloat16), preferred_element_type=jnp.float32
        ).astype(jnp.bfloat16).reshape(2, half, chans)
        to_mate(row).start()

    def pair(row):
        to_mate(row).wait()
        total = fp_ref[row, core].astype(jnp.float32) + recv_a[row].astype(jnp.float32)
        send_b[row] = total.astype(jnp.bfloat16).reshape(chips, group, chans)
        for off in range(1, chips):
            to_chip(row, off).start()

    def edge(index):
        return jnp.where(index < HALO, index, rows - 2 * HALO + index)

    @pl.loop(HALO, rows + HALO)
    def _(row):
        mix(row)

    @pl.loop(HALO, rows - HALO)
    def _(row):
        conv(row)

    for copy in across:
        copy.wait()

    @pl.loop(0, 2 * HALO)
    def _(index):
        mix(jnp.where(index < HALO, index, rows + index))

    @pl.loop(HALO, rows - HALO)
    def _(row):
        pair(row)

    @pl.loop(0, 2 * HALO)
    def _(index):
        conv(edge(index))

    @pl.loop(0, 2 * HALO)
    def _(index):
        pair(edge(index))

    for row in list(range(HALO, rows - HALO)) + list(range(HALO)) + list(range(rows - HALO, rows)):
        total = send_b[row, chip].astype(jnp.float32)
        for off in range(1, chips):
            to_chip(row, off).wait()
            total = total + recv_b[off - 1, row].astype(jnp.float32)
        red[:, row, :] = total
    for d in range(lat_n):
        snd2[d] = red[d * count : (d + 1) * count].reshape(count * rows, chans).astype(wire)

    second = []
    for off in range(1, lat_n):
        peer = lax.rem(lat + off, lat_n)
        copy = remote(
            snd2.at[peer], recv2.at[lat], s2.at[off - 1], r2.at[off - 1], (peer, lon)
        )
        copy.start()
        second.append(copy)
    recv2[lat] = snd2[lat]
    quad_weight = (math.pi / nlat) * jnp.sin(
        (lax.broadcasted_iota(jnp.int32, (1, nlat), 1).astype(jnp.float32) + 0.5) * math.pi / nlat
    )
    tables = [legendre[:, t, :] for t in range(count)]
    for copy in second:
        copy.wait()

    for t in range(count):
        cells = recv2[:, t * rows : (t + 1) * rows, :].astype(jnp.float32)
        cells = cells.reshape(lat_n * rows, chans).astype(jnp.bfloat16)
        analysis = (tables[t] * quad_weight).astype(jnp.bfloat16)
        spectra = jnp.dot(analysis, cells, preferred_element_type=jnp.float32)
        filtered = (spectra * filt_ref[...]).astype(jnp.bfloat16)
        result = jnp.dot(
            tables[t].T.astype(jnp.bfloat16), filtered, preferred_element_type=jnp.float32
        )
        back[:, t * rows : (t + 1) * rows, :] = result.reshape(lat_n, rows, chans)
    for d in range(lat_n):
        snd3[d] = back[d].astype(wire)

    third = []
    for off in range(1, lat_n):
        peer = lax.rem(lat + off, lat_n)
        copy = remote(
            snd3.at[peer], out_ref.at[place, lat], s3.at[off - 1], r3.at[off - 1], (peer, lon)
        )
        copy.start()
        third.append(copy)
    out_ref[place, lat] = snd3[lat]

    last = []

    def spread(slot):
        source = lax.rem(lat + lat_n - slot, lat_n)
        block = out_ref.at[place, source]
        hops = []
        for off in range(1, chips):
            peer = lax.rem(chip + off, chips)
            hops.append(
                remote(
                    block, block, sx.at[slot, off - 1], rx.at[slot, off - 1],
                    (lat, peer * 2 + core),
                )
            )
            hops[-1].start()
        last.append(remote(block, block, sp.at[slot], rp.at[slot], (lat, mate)))
        last[-1].start()
        return hops

    def forward_on(slot, hops):
        source = lax.rem(lat + lat_n - slot, lat_n)
        for off in range(1, chips):
            hops[off - 1].wait()
            origin = core * chips + lax.rem(chip + chips - off, chips)
            block = out_ref.at[origin, source]
            last.append(
                remote(block, block, sf.at[slot, off - 1], rf.at[slot, off - 1], (lat, mate))
            )
            last[-1].start()

    hops = {}
    for slot in range(lat_n):
        if slot:
            third[slot - 1].wait()
        hops[slot] = spread(slot)
        if slot >= 3:
            forward_on(slot - 3, hops[slot - 3])
    for slot in range(max(lat_n - 3, 0), lat_n):
        forward_on(slot, hops[slot])
    for copy in last:
        copy.wait()


def output_kernel(syn_ref, ac_ref, table_ref, mix_ref, o_ref, wide):
    rows, width, chans = ac_ref.shape
    all_q = table_ref.shape[1]
    wide[...] = syn_ref[...].astype(jnp.float32).reshape(all_q, rows, chans)
    for row in range(rows):
        waves = wide[:, row, :].astype(jnp.bfloat16)
        field = jnp.dot(table_ref[...], waves, preferred_element_type=jnp.float32)
        active = jax.nn.gelu(field, approximate=True).astype(jnp.bfloat16)
        total = ac_ref[row] + jnp.dot(active, mix_ref[...], preferred_element_type=jnp.float32)
        o_ref[:, row, :] = total.T


def per_device(
    grid_field,
    disco_dlat,
    disco_dlon,
    disco_basis,
    disco_quad,
    disco_weight,
    norm_gain,
    spectral_filter,
    mix_weight,
):
    lat_n = lax.axis_size("lat")
    lon_n = lax.axis_size("lon")
    chans, rows, width = grid_field.shape
    nlat, nlon = rows * lat_n, width * lon_n
    modes = M_DEV * lat_n
    all_q = 2 * modes
    degrees = spectral_filter.shape[1]
    group = all_q // lon_n
    count = group // lat_n
    basis_count = disco_weight.shape[0]
    f32, bf16 = jnp.float32, jnp.bfloat16

    wire = bf16 if (count * rows) % 16 == 0 else f32
    block = (lat_n, count * rows, chans)
    chips = lon_n // 2
    tall = width + 2 * PAD
    dma = pltpu.SemaphoreType.DMA
    vmem = pltpu.VMEM
    synthesis, after_conv, inverse = pl.pallas_call(
        functools.partial(field_kernel, lat_n, lon_n, modes),
        out_shape=(
            jax.ShapeDtypeStruct((lon_n,) + block, wire),
            jax.ShapeDtypeStruct((rows, width, chans), f32),
            jax.ShapeDtypeStruct((width, all_q), bf16),
        ),
        in_specs=[SM] * 4 + [VM] * 4,
        out_specs=(VM, VM, VM),
        scratch_shapes=[
            vmem((rows + 2 * HALO, tall, chans), bf16),
            vmem(
                ((basis_count + 1) // 2, rows + 2 * HALO, chans // LANES, 2 * tall, LANES), f32
            ),
            vmem((all_q, width), bf16),
            vmem((rows, 2, all_q // 2, chans), bf16),
            vmem((rows, all_q // 2, chans), bf16),
            vmem((rows, chips, group, chans), bf16),
            vmem((chips - 1, rows, group, chans), bf16),
            vmem((group, rows, chans), f32),
            vmem(block, wire),
            vmem(block, wire),
            vmem((degrees, count, nlat), f32),
            vmem((2, count, nlat), f32),
            vmem(block, f32),
            vmem(block, wire),
            dma((9,)), dma((9,)),
            dma((rows,)), dma((rows,)),
            dma((rows, chips - 1)), dma((rows, chips - 1)),
            dma((lat_n - 1,)), dma((lat_n - 1,)),
            dma((lat_n - 1,)), dma((lat_n - 1,)),
            dma((lat_n, chips - 1)), dma((lat_n, chips - 1)),
            dma((lat_n,)), dma((lat_n,)),
            dma((lat_n, chips - 1)), dma((lat_n, chips - 1)),
        ],
        compiler_params=pltpu.CompilerParams(collective_id=0, has_side_effects=True),
    )(
        disco_dlat, disco_dlon, disco_basis, disco_quad,
        grid_field, disco_weight, norm_gain[None, :], spectral_filter.T,
    )

    return pl.pallas_call(
        output_kernel,
        out_shape=jax.ShapeDtypeStruct((chans, rows, width), f32),
        in_specs=[VM] * 4,
        out_specs=VM,
        scratch_shapes=[pltpu.VMEM((all_q, rows, chans), f32)],
    )(synthesis, after_conv, inverse, mix_weight)


def solution(mesh):
    placed = (
        P(None, "lat", "lon"),
        P("lat", None),
        P("lat", None),
        P("lat", None),
        P("lat", None),
        P(),
        P(),
        P(),
        P(),
    )
    return jax.shard_map(
        per_device, mesh=mesh, in_specs=placed, out_specs=P(None, "lat", "lon"), check_vma=False
    )
```

```python
import functools
import math

import jax
import jax.numpy as jnp
from jax import lax
from jax.experimental import pallas as pl
from jax.experimental.pallas import tpu as pltpu
from jax.sharding import PartitionSpec as P

M_DEV = 8
HALO = 2
PAD = 16
LANES = 128
MESH = pl.DeviceIdType.MESH
VM = pl.BlockSpec(memory_space=pltpu.VMEM)
SM = pl.BlockSpec(memory_space=pltpu.SMEM)
HB = pl.BlockSpec(memory_space=pl.ANY)


def order_tables(forward_ref, inverse_ref, lon, nlon):
    width, all_q = inverse_ref.shape

    def wave(shape, q_axis):
        q = lax.broadcasted_iota(jnp.int32, shape, q_axis)
        j = lax.broadcasted_iota(jnp.int32, shape, 1 - q_axis) + lon * width
        turns = (j * (q >> 1) + (q & 1) * (nlon // 4)).astype(jnp.float32)
        turns = turns - nlon * jnp.floor(turns * (1.0 / nlon))
        return q, jnp.cos(turns * (2.0 * math.pi / nlon))

    q, cells = wave((all_q, width), 0)
    forward_ref[...] = (cells * (2.0 * math.pi / nlon)).astype(forward_ref.dtype)
    q, cells = wave((width, all_q), 1)
    inverse_ref[...] = (cells * jnp.where(q < 2, 1.0, 2.0)).astype(inverse_ref.dtype)


def legendre_table(table_ref, start_ref, first_q, modes):
    degrees, count, nlat = table_ref.shape
    shape = (count, nlat)

    def order_of(dims):
        q = lax.broadcasted_iota(jnp.int32, dims, 0) + first_q
        return (q >> 1).astype(jnp.float32)

    order = order_of(shape)
    colatitude = (
        (lax.broadcasted_iota(jnp.int32, shape, 1).astype(jnp.float32) + 0.5) * math.pi / nlat
    )
    cosine, sine = jnp.cos(colatitude), jnp.sin(colatitude)
    counters = lax.broadcasted_iota(jnp.int32, (count, modes), 1).astype(jnp.float32) + 1.0
    logs = jnp.log((2.0 * counters - 1.0) / (2.0 * counters))
    logs = jnp.where(counters <= order_of((count, modes)), logs, 0.0)
    log_product = jnp.sum(logs, axis=1, keepdims=True)
    log_seed = 0.5 * (
        jnp.log((2.0 * order + 1.0) / (4.0 * math.pi)) + log_product
    ) + order * jnp.log(sine)
    rescale = jnp.clip(-log_seed, 0.0, 80.0)
    seed = jnp.exp(log_seed + rescale)
    undo = jnp.exp(-rescale)
    square = order * order
    start_ref[...] = jnp.zeros(start_ref.shape, jnp.float32)

    def advance(degree, pair):
        previous, older = pair
        ell = degree.astype(jnp.float32)
        a = jnp.sqrt(
            jnp.maximum(4.0 * ell * ell - 1.0, 1.0) / jnp.maximum(ell * ell - square, 1.0)
        )
        below = (ell - 1.0) * (ell - 1.0)
        b = jnp.sqrt(jnp.maximum(below - square, 0.0) / jnp.maximum(4.0 * below - 1.0, 1.0))
        current = jnp.where(
            order == ell, seed, jnp.where(ell > order, a * (cosine * previous - b * older), 0.0)
        )
        table_ref[degree] = current * undo
        return (current, previous)

    lax.fori_loop(0, degrees, advance, (start_ref[0], start_ref[1]), unroll=4)


def field_kernel(
    lat_n, lon_n, modes,
    dlat_ref, dlon_ref, basis_ref, quad_ref, x_hbm, w_hbm, gain_ref, filt_ref,
    out_ref, ac_hbm, inverse_ref,
    x_ref, w_ref, ac_ref, load_x, load_w, store_ac,
    xp_ref, y_ref, forward, fp_ref, recv_a, send_b, recv_b, red, snd2, recv2,
    legendre, start, back, snd3,
    halo_s, halo_r, sa, ra, sb, rb, s2, r2, s3, r3, sx, rx, sp, rp, sf, rf,
):
    rows, width, chans = ac_ref.shape
    basis_count = w_ref.shape[0]
    taps = dlat_ref.shape[1]
    slabs = chans // LANES
    tall = xp_ref.shape[1]
    all_q = forward.shape[0]
    half = all_q // 2
    chips = lon_n // 2
    group = all_q // lon_n
    count = group // lat_n
    nlat, nlon = lat_n * rows, lon_n * width
    wire = snd2.dtype
    lat, lon = lax.axis_index("lat"), lax.axis_index("lon")
    up, down = lax.rem(lat + lat_n - 1, lat_n), lax.rem(lat + 1, lat_n)
    left, right = lax.rem(lon + lon_n - 1, lon_n), lax.rem(lon + 1, lon_n)
    chip, core = lon // 2, lax.rem(lon, 2)
    mate = chip * 2 + 1 - core

    def remote(source, target, send, recv, peer):
        return pltpu.make_async_remote_copy(
            src_ref=source, dst_ref=target, send_sem=send, recv_sem=recv,
            device_id=peer, device_id_type=MESH,
        )

    barrier = pltpu.get_barrier_semaphore()
    peers = [(lax.rem(lat + off, lat_n), lon) for off in range(1, lat_n)]
    peers += [(lat, lax.rem(lon + off, lon_n)) for off in range(1, lon_n)]
    peers += [(a, b) for a in (up, down) for b in (left, right)]
    for peer in peers:
        pl.semaphore_signal(barrier, inc=1, device_id=peer, device_id_type=MESH)

    loads = []
    for c in range(slabs):
        part = slice(c * LANES, (c + 1) * LANES)
        loads.append(pltpu.make_async_copy(x_hbm.at[part], x_ref.at[part], load_x.at[c]))
        loads[-1].start()
    weights = pltpu.make_async_copy(w_hbm, w_ref, load_w)
    weights.start()

    def turn(row, c):
        part = slice(c * LANES, (c + 1) * LANES)
        cells = x_ref[part, row, :].T
        ac_ref[row, :, part] = cells
        xp_ref[row + HALO, PAD : PAD + width, part] = cells.astype(jnp.bfloat16)

    row_spans = {-1: (HALO, rows + HALO, HALO), 0: (HALO, HALO, rows), 1: (rows, 0, HALO)}
    col_spans = {-1: (PAD, PAD + width, PAD), 0: (PAD, PAD, width), 1: (width, 0, PAD)}

    def halo(dv, dh):
        peer = ({-1: up, 0: lat, 1: down}[dv], {-1: left, 0: lon, 1: right}[dh])
        rs, rd, rn = row_spans[dv]
        cs, cd, cn = col_spans[dh]
        index = (dv + 1) * 3 + dh + 1
        return remote(
            xp_ref.at[rs : rs + rn, cs : cs + cn, :],
            xp_ref.at[rd : rd + rn, cd : cd + cn, :],
            halo_s.at[index], halo_r.at[index], peer,
        )

    for c in range(slabs):
        loads[c].wait()
        for row in list(range(HALO)) + list(range(rows - HALO, rows)):
            turn(row, c)
    pl.semaphore_wait(barrier, len(peers))
    across = [halo(dv, dh) for dv in (-1, 1) for dh in (0, -1, 1)]
    for copy in across:
        copy.start()
    for row in range(HALO, rows - HALO):
        for c in range(slabs):
            turn(row, c)
    beside = [halo(0, dh) for dh in (-1, 1)]
    for copy in beside:
        copy.start()

    order_tables(forward, inverse_ref, lon, nlon)
    place = core * chips + chip
    legendre_table(legendre, start, place * group + lat * count, modes)
    weights.wait()
    for copy in beside:
        copy.wait()

    def mix(row):
        cells = xp_ref[row]
        for b in range(basis_count):
            mixed = jnp.dot(cells, w_ref[b], preferred_element_type=jnp.float32)
            for c in range(slabs):
                y_ref[b // 2, row, c, pl.ds(b % 2, tall, stride=2), :] = mixed[
                    :, c * LANES : (c + 1) * LANES
                ]

    step = 32

    def to_mate(row):
        return remote(
            fp_ref.at[row, 1 - core], recv_a.at[row], sa.at[row], ra.at[row], (lat, mate)
        )

    def to_chip(row, off):
        peer = lax.rem(chip + off, chips)
        return remote(
            send_b.at[row, peer], recv_b.at[off - 1, row],
            sb.at[row, off - 1], rb.at[row, off - 1], (lat, peer * 2 + core),
        )

    def put(row):
        return pltpu.make_async_copy(ac_ref.at[row], ac_hbm.at[row], store_ac.at[row])

    def conv(row):
        @pl.loop(0, width // step)
        def _(part):
            base = pl.multiple_of(part * step, step)
            totals = [
                ac_ref[row, pl.ds(base, step), c * LANES : (c + 1) * LANES] for c in range(slabs)
            ]
            for k in range(taps):
                basis = basis_ref[row, k]
                source = row + dlat_ref[row, k]
                globally = source + lat * rows
                inside = jnp.logical_and(globally >= 0, globally < nlat)
                scale = jnp.where(inside, quad_ref[row, k], 0.0)
                begin = 2 * (base + dlon_ref[row, k] + PAD) + (basis & 1)
                for c in range(slabs):
                    totals[c] = totals[c] + scale * y_ref[
                        basis >> 1, source + HALO, c, pl.ds(begin, step, stride=2), :
                    ]
            for c in range(slabs):
                ac_ref[row, pl.ds(base, step), c * LANES : (c + 1) * LANES] = totals[c]

        put(row).start()
        cells = ac_ref[row]
        mean = jnp.mean(cells * cells, axis=1, keepdims=True)
        normed = cells * lax.rsqrt(mean + 1e-06) * gain_ref[...][None, :]
        fp_ref[row] = jnp.dot(
            forward[...], normed.astype(jnp.bfloat16), preferred_element_type=jnp.float32
        ).astype(jnp.bfloat16).reshape(2, half, chans)
        to_mate(row).start()

    def pair(row):
        to_mate(row).wait()
        total = fp_ref[row, core].astype(jnp.float32) + recv_a[row].astype(jnp.float32)
        send_b[row] = total.astype(jnp.bfloat16).reshape(chips, group, chans)
        for off in range(1, chips):
            to_chip(row, off).start()

    def edge(index):
        return jnp.where(index < HALO, index, rows - 2 * HALO + index)

    @pl.loop(HALO, rows + HALO)
    def _(row):
        mix(row)

    @pl.loop(HALO, rows - HALO)
    def _(row):
        conv(row)

    @pl.loop(HALO, rows - HALO)
    def _(row):
        pair(row)

    for copy in across:
        copy.wait()

    @pl.loop(0, 2 * HALO)
    def _(index):
        mix(jnp.where(index < HALO, index, rows + index))

    @pl.loop(0, 2 * HALO)
    def _(index):
        conv(edge(index))

    @pl.loop(0, 2 * HALO)
    def _(index):
        pair(edge(index))

    for row in list(range(HALO, rows - HALO)) + list(range(HALO)) + list(range(rows - HALO, rows)):
        total = send_b[row, chip].astype(jnp.float32)
        for off in range(1, chips):
            to_chip(row, off).wait()
            total = total + recv_b[off - 1, row].astype(jnp.float32)
        red[:, row, :] = total
    for d in range(lat_n):
        snd2[d] = red[d * count : (d + 1) * count].reshape(count * rows, chans).astype(wire)

    second = []
    for off in range(1, lat_n):
        peer = lax.rem(lat + off, lat_n)
        copy = remote(
            snd2.at[peer], recv2.at[lat], s2.at[off - 1], r2.at[off - 1], (peer, lon)
        )
        copy.start()
        second.append(copy)
    recv2[lat] = snd2[lat]
    quad_weight = (math.pi / nlat) * jnp.sin(
        (lax.broadcasted_iota(jnp.int32, (1, nlat), 1).astype(jnp.float32) + 0.5) * math.pi / nlat
    )
    tables = [legendre[:, t, :] for t in range(count)]
    for copy in second:
        copy.wait()

    for t in range(count):
        cells = recv2[:, t * rows : (t + 1) * rows, :].astype(jnp.float32)
        cells = cells.reshape(lat_n * rows, chans).astype(jnp.bfloat16)
        analysis = (tables[t] * quad_weight).astype(jnp.bfloat16)
        spectra = jnp.dot(analysis, cells, preferred_element_type=jnp.float32)
        filtered = (spectra * filt_ref[...]).astype(jnp.bfloat16)
        result = jnp.dot(
            tables[t].T.astype(jnp.bfloat16), filtered, preferred_element_type=jnp.float32
        )
        back[:, t * rows : (t + 1) * rows, :] = result.reshape(lat_n, rows, chans)
    for d in range(lat_n):
        snd3[d] = back[d].astype(wire)

    third = []
    for off in range(1, lat_n):
        peer = lax.rem(lat + off, lat_n)
        copy = remote(
            snd3.at[peer], out_ref.at[place, lat], s3.at[off - 1], r3.at[off - 1], (peer, lon)
        )
        copy.start()
        third.append(copy)
    out_ref[place, lat] = snd3[lat]

    last = []

    def spread(slot):
        source = lax.rem(lat + lat_n - slot, lat_n)
        block = out_ref.at[place, source]
        hops = []
        for off in range(1, chips):
            peer = lax.rem(chip + off, chips)
            hops.append(
                remote(
                    block, block, sx.at[slot, off - 1], rx.at[slot, off - 1],
                    (lat, peer * 2 + core),
                )
            )
            hops[-1].start()
        last.append(remote(block, block, sp.at[slot], rp.at[slot], (lat, mate)))
        last[-1].start()
        return hops

    def forward_on(slot, hops):
        source = lax.rem(lat + lat_n - slot, lat_n)
        for off in range(1, chips):
            hops[off - 1].wait()
            origin = core * chips + lax.rem(chip + chips - off, chips)
            block = out_ref.at[origin, source]
            last.append(
                remote(block, block, sf.at[slot, off - 1], rf.at[slot, off - 1], (lat, mate))
            )
            last[-1].start()

    hops = {}
    for slot in range(lat_n):
        if slot:
            third[slot - 1].wait()
        hops[slot] = spread(slot)
        if slot >= 3:
            forward_on(slot - 3, hops[slot - 3])
    for slot in range(max(lat_n - 3, 0), lat_n):
        forward_on(slot, hops[slot])
    for copy in last:
        copy.wait()
    for row in range(rows):
        put(row).wait()


def output_kernel(syn_ref, ac_ref, table_ref, mix_ref, o_ref, wide, active):
    rows, width, _ = ac_ref.shape
    all_q = table_ref.shape[1]
    chans = mix_ref.shape[0]

    @pl.when(pl.program_id(0) == 0)
    def _():
        wide[...] = syn_ref[...].astype(jnp.float32).reshape(all_q, rows, chans)
        for row in range(rows):
            waves = wide[:, row, :].astype(jnp.bfloat16)
            field = jnp.dot(table_ref[...], waves, preferred_element_type=jnp.float32)
            active[row] = jax.nn.gelu(field, approximate=True).astype(jnp.bfloat16)

    for row in range(rows):
        total = ac_ref[row] + jnp.dot(
            active[row], mix_ref[...], preferred_element_type=jnp.float32
        )
        o_ref[:, row, :] = total.T


def per_device(
    grid_field,
    disco_dlat,
    disco_dlon,
    disco_basis,
    disco_quad,
    disco_weight,
    norm_gain,
    spectral_filter,
    mix_weight,
):
    lat_n = lax.axis_size("lat")
    lon_n = lax.axis_size("lon")
    chans, rows, width = grid_field.shape
    nlat, nlon = rows * lat_n, width * lon_n
    modes = M_DEV * lat_n
    all_q = 2 * modes
    degrees = spectral_filter.shape[1]
    group = all_q // lon_n
    count = group // lat_n
    basis_count = disco_weight.shape[0]
    f32, bf16 = jnp.float32, jnp.bfloat16

    wire = bf16 if (count * rows) % 16 == 0 else f32
    block = (lat_n, count * rows, chans)
    chips = lon_n // 2
    tall = width + 2 * PAD
    dma = pltpu.SemaphoreType.DMA
    vmem = pltpu.VMEM
    synthesis, after_conv, inverse = pl.pallas_call(
        functools.partial(field_kernel, lat_n, lon_n, modes),
        out_shape=(
            jax.ShapeDtypeStruct((lon_n,) + block, wire),
            jax.ShapeDtypeStruct((rows, width, chans), f32),
            jax.ShapeDtypeStruct((width, all_q), bf16),
        ),
        in_specs=[SM] * 4 + [HB, HB, VM, VM],
        out_specs=(VM, HB, VM),
        scratch_shapes=[
            vmem((chans, rows, width), f32),
            vmem(disco_weight.shape, bf16),
            vmem((rows, width, chans), f32),
            dma((chans // LANES,)), dma, dma((rows,)),
            vmem((rows + 2 * HALO, tall, chans), bf16),
            vmem(
                ((basis_count + 1) // 2, rows + 2 * HALO, chans // LANES, 2 * tall, LANES), f32
            ),
            vmem((all_q, width), bf16),
            vmem((rows, 2, all_q // 2, chans), bf16),
            vmem((rows, all_q // 2, chans), bf16),
            vmem((rows, chips, group, chans), bf16),
            vmem((chips - 1, rows, group, chans), bf16),
            vmem((group, rows, chans), f32),
            vmem(block, wire),
            vmem(block, wire),
            vmem((degrees, count, nlat), f32),
            vmem((2, count, nlat), f32),
            vmem(block, f32),
            vmem(block, wire),
            dma((9,)), dma((9,)),
            dma((rows,)), dma((rows,)),
            dma((rows, chips - 1)), dma((rows, chips - 1)),
            dma((lat_n - 1,)), dma((lat_n - 1,)),
            dma((lat_n - 1,)), dma((lat_n - 1,)),
            dma((lat_n, chips - 1)), dma((lat_n, chips - 1)),
            dma((lat_n,)), dma((lat_n,)),
            dma((lat_n, chips - 1)), dma((lat_n, chips - 1)),
        ],
        compiler_params=pltpu.CompilerParams(collective_id=0, has_side_effects=True),
    )(
        disco_dlat, disco_dlon, disco_basis, disco_quad,
        grid_field, disco_weight, norm_gain, spectral_filter.T,
    )

    whole = lambda shape: pl.BlockSpec(shape, lambda o: (0,) * len(shape))
    return pl.pallas_call(
        output_kernel,
        grid=(chans // LANES,),
        out_shape=jax.ShapeDtypeStruct((chans, rows, width), f32),
        in_specs=[
            whole(synthesis.shape),
            pl.BlockSpec((rows, width, LANES), lambda o: (0, 0, o)),
            whole(inverse.shape),
            pl.BlockSpec((chans, LANES), lambda o: (0, o)),
        ],
        out_specs=pl.BlockSpec((LANES, rows, width), lambda o: (o, 0, 0)),
        scratch_shapes=[vmem((all_q, rows, chans), f32), vmem((rows, width, chans), bf16)],
    )(synthesis, after_conv, inverse, mix_weight)


def solution(mesh):
    placed = (
        P(None, "lat", "lon"),
        P("lat", None),
        P("lat", None),
        P("lat", None),
        P("lat", None),
        P(),
        P(),
        P(),
        P(),
    )
    return jax.shard_map(
        per_device, mesh=mesh, in_specs=placed, out_specs=P(None, "lat", "lon"), check_vma=False
    )
```

```python
import functools
import math

import jax
import jax.numpy as jnp
from jax import lax
from jax.experimental import pallas as pl
from jax.experimental.pallas import tpu as pltpu
from jax.sharding import PartitionSpec as P

M_DEV = 8
HALO = 2
PAD = 16
LANES = 128
MESH = pl.DeviceIdType.MESH
VM = pl.BlockSpec(memory_space=pltpu.VMEM)
SM = pl.BlockSpec(memory_space=pltpu.SMEM)
HB = pl.BlockSpec(memory_space=pl.ANY)


def order_tables(forward_ref, inverse_ref, lon, nlon):
    width, all_q = inverse_ref.shape

    def wave(shape, q_axis):
        q = lax.broadcasted_iota(jnp.int32, shape, q_axis)
        j = lax.broadcasted_iota(jnp.int32, shape, 1 - q_axis) + lon * width
        turns = (j * (q >> 1) + (q & 1) * (nlon // 4)).astype(jnp.float32)
        turns = turns - nlon * jnp.floor(turns * (1.0 / nlon))
        return q, jnp.cos(turns * (2.0 * math.pi / nlon))

    q, cells = wave((all_q, width), 0)
    forward_ref[...] = (cells * (2.0 * math.pi / nlon)).astype(forward_ref.dtype)
    q, cells = wave((width, all_q), 1)
    inverse_ref[...] = (cells * jnp.where(q < 2, 1.0, 2.0)).astype(inverse_ref.dtype)


def legendre_table(table_ref, start_ref, first_q, modes):
    degrees, count, nlat = table_ref.shape
    shape = (count, nlat)

    def order_of(dims):
        q = lax.broadcasted_iota(jnp.int32, dims, 0) + first_q
        return (q >> 1).astype(jnp.float32)

    order = order_of(shape)
    colatitude = (
        (lax.broadcasted_iota(jnp.int32, shape, 1).astype(jnp.float32) + 0.5) * math.pi / nlat
    )
    cosine, sine = jnp.cos(colatitude), jnp.sin(colatitude)
    counters = lax.broadcasted_iota(jnp.int32, (count, modes), 1).astype(jnp.float32) + 1.0
    logs = jnp.log((2.0 * counters - 1.0) / (2.0 * counters))
    logs = jnp.where(counters <= order_of((count, modes)), logs, 0.0)
    log_product = jnp.sum(logs, axis=1, keepdims=True)
    log_seed = 0.5 * (
        jnp.log((2.0 * order + 1.0) / (4.0 * math.pi)) + log_product
    ) + order * jnp.log(sine)
    rescale = jnp.clip(-log_seed, 0.0, 80.0)
    seed = jnp.exp(log_seed + rescale)
    undo = jnp.exp(-rescale)
    square = order * order
    start_ref[...] = jnp.zeros(start_ref.shape, jnp.float32)

    def advance(degree, pair):
        previous, older = pair
        ell = degree.astype(jnp.float32)
        a = jnp.sqrt(
            jnp.maximum(4.0 * ell * ell - 1.0, 1.0) / jnp.maximum(ell * ell - square, 1.0)
        )
        below = (ell - 1.0) * (ell - 1.0)
        b = jnp.sqrt(jnp.maximum(below - square, 0.0) / jnp.maximum(4.0 * below - 1.0, 1.0))
        current = jnp.where(
            order == ell, seed, jnp.where(ell > order, a * (cosine * previous - b * older), 0.0)
        )
        table_ref[degree] = current * undo
        return (current, previous)

    lax.fori_loop(0, degrees, advance, (start_ref[0], start_ref[1]), unroll=4)


def field_kernel(
    lat_n, lon_n, modes,
    dlat_ref, dlon_ref, basis_ref, quad_ref, x_hbm, w_hbm, gain_ref, filt_ref,
    out_ref, ac_hbm, inverse_ref,
    x_ref, w_ref, ac_ref, load_x, load_w, store_ac,
    xp_ref, y_ref, forward, fp_ref, recv_a, send_b, recv_b, red, snd2, recv2,
    legendre, start, back, snd3,
    halo_s, halo_r, sa, ra, sb, rb, s2, r2, s3, r3, sx, rx, sp, rp, sf, rf,
):
    rows, width, chans = ac_ref.shape
    basis_count = w_ref.shape[0]
    taps = dlat_ref.shape[1]
    slabs = chans // LANES
    tall = xp_ref.shape[1]
    all_q = forward.shape[0]
    half = all_q // 2
    chips = lon_n // 2
    group = all_q // lon_n
    count = group // lat_n
    nlat, nlon = lat_n * rows, lon_n * width
    wire = snd2.dtype
    lat, lon = lax.axis_index("lat"), lax.axis_index("lon")
    up, down = lax.rem(lat + lat_n - 1, lat_n), lax.rem(lat + 1, lat_n)
    left, right = lax.rem(lon + lon_n - 1, lon_n), lax.rem(lon + 1, lon_n)
    chip, core = lon // 2, lax.rem(lon, 2)
    mate = chip * 2 + 1 - core

    def remote(source, target, send, recv, peer):
        return pltpu.make_async_remote_copy(
            src_ref=source, dst_ref=target, send_sem=send, recv_sem=recv,
            device_id=peer, device_id_type=MESH,
        )

    barrier = pltpu.get_barrier_semaphore()
    peers = [(lax.rem(lat + off, lat_n), lon) for off in range(1, lat_n)]
    peers += [(lat, lax.rem(lon + off, lon_n)) for off in range(1, lon_n)]
    peers += [(a, b) for a in (up, down) for b in (left, right)]
    for peer in peers:
        pl.semaphore_signal(barrier, inc=1, device_id=peer, device_id_type=MESH)

    loads = []
    for c in range(slabs):
        part = slice(c * LANES, (c + 1) * LANES)
        loads.append(pltpu.make_async_copy(x_hbm.at[part], x_ref.at[part], load_x.at[c]))
        loads[-1].start()
    weights = pltpu.make_async_copy(w_hbm, w_ref, load_w)
    weights.start()

    def turn(row, c):
        part = slice(c * LANES, (c + 1) * LANES)
        cells = x_ref[part, row, :].T
        ac_ref[row, :, part] = cells
        xp_ref[row + HALO, PAD : PAD + width, part] = cells.astype(jnp.bfloat16)

    row_spans = {-1: (HALO, rows + HALO, HALO), 0: (HALO, HALO, rows), 1: (rows, 0, HALO)}
    col_spans = {-1: (PAD, PAD + width, PAD), 0: (PAD, PAD, width), 1: (width, 0, PAD)}

    def halo(dv, dh):
        peer = ({-1: up, 0: lat, 1: down}[dv], {-1: left, 0: lon, 1: right}[dh])
        rs, rd, rn = row_spans[dv]
        cs, cd, cn = col_spans[dh]
        index = (dv + 1) * 3 + dh + 1
        return remote(
            xp_ref.at[rs : rs + rn, cs : cs + cn, :],
            xp_ref.at[rd : rd + rn, cd : cd + cn, :],
            halo_s.at[index], halo_r.at[index], peer,
        )

    for c in range(slabs):
        loads[c].wait()
        for row in list(range(HALO)) + list(range(rows - HALO, rows)):
            turn(row, c)
    pl.semaphore_wait(barrier, len(peers))
    across = [halo(dv, dh) for dv in (-1, 1) for dh in (0, -1, 1)]
    for copy in across:
        copy.start()
    for row in range(HALO, rows - HALO):
        for c in range(slabs):
            turn(row, c)
    beside = [halo(0, dh) for dh in (-1, 1)]
    for copy in beside:
        copy.start()

    order_tables(forward, inverse_ref, lon, nlon)
    place = core * chips + chip
    legendre_table(legendre, start, place * group + lat * count, modes)
    weights.wait()
    for copy in beside:
        copy.wait()

    def mix(row):
        cells = xp_ref[row]
        for b in range(basis_count):
            mixed = jnp.dot(cells, w_ref[b], preferred_element_type=jnp.float32)
            for c in range(slabs):
                y_ref[b // 2, row, c, pl.ds(b % 2, tall, stride=2), :] = mixed[
                    :, c * LANES : (c + 1) * LANES
                ]

    step = 64

    def to_mate(row):
        return remote(
            fp_ref.at[row, 1 - core], recv_a.at[row], sa.at[row], ra.at[row], (lat, mate)
        )

    def to_chip(row, off):
        peer = lax.rem(chip + off, chips)
        return remote(
            send_b.at[row, peer], recv_b.at[off - 1, row],
            sb.at[row, off - 1], rb.at[row, off - 1], (lat, peer * 2 + core),
        )

    def put(row):
        return pltpu.make_async_copy(ac_ref.at[row], ac_hbm.at[row], store_ac.at[row])

    def conv(row):
        @pl.loop(0, width // step)
        def _(part):
            base = pl.multiple_of(part * step, step)
            totals = [
                ac_ref[row, pl.ds(base, step), c * LANES : (c + 1) * LANES] for c in range(slabs)
            ]
            for k in range(taps):
                basis = basis_ref[row, k]
                source = row + dlat_ref[row, k]
                globally = source + lat * rows
                inside = jnp.logical_and(globally >= 0, globally < nlat)
                scale = jnp.where(inside, quad_ref[row, k], 0.0)
                begin = 2 * (base + dlon_ref[row, k] + PAD) + (basis & 1)
                for c in range(slabs):
                    totals[c] = totals[c] + scale * y_ref[
                        basis >> 1, source + HALO, c, pl.ds(begin, step, stride=2), :
                    ]
            for c in range(slabs):
                ac_ref[row, pl.ds(base, step), c * LANES : (c + 1) * LANES] = totals[c]

        put(row).start()
        cells = ac_ref[row]
        mean = jnp.mean(cells * cells, axis=1, keepdims=True)
        normed = cells * lax.rsqrt(mean + 1e-06) * gain_ref[...][None, :]
        fp_ref[row] = jnp.dot(
            forward[...], normed.astype(jnp.bfloat16), preferred_element_type=jnp.float32
        ).astype(jnp.bfloat16).reshape(2, half, chans)
        to_mate(row).start()

    def pair(row):
        to_mate(row).wait()
        total = fp_ref[row, core].astype(jnp.float32) + recv_a[row].astype(jnp.float32)
        send_b[row] = total.astype(jnp.bfloat16).reshape(chips, group, chans)
        for off in range(1, chips):
            to_chip(row, off).start()

    def edge(index):
        return jnp.where(index < HALO, index, rows - 2 * HALO + index)

    @pl.loop(HALO, rows + HALO, unroll=2)
    def _(row):
        mix(row)

    @pl.loop(HALO, rows - HALO)
    def _(row):
        conv(row)

    @pl.loop(HALO, rows - HALO)
    def _(row):
        pair(row)

    for copy in across:
        copy.wait()

    @pl.loop(0, 2 * HALO, unroll=2)
    def _(index):
        mix(jnp.where(index < HALO, index, rows + index))

    @pl.loop(0, 2 * HALO)
    def _(index):
        conv(edge(index))

    @pl.loop(0, 2 * HALO)
    def _(index):
        pair(edge(index))

    for row in list(range(HALO, rows - HALO)) + list(range(HALO)) + list(range(rows - HALO, rows)):
        total = send_b[row, chip].astype(jnp.float32)
        for off in range(1, chips):
            to_chip(row, off).wait()
            total = total + recv_b[off - 1, row].astype(jnp.float32)
        red[:, row, :] = total
    for d in range(lat_n):
        snd2[d] = red[d * count : (d + 1) * count].reshape(count * rows, chans).astype(wire)

    second = []
    for off in range(1, lat_n):
        peer = lax.rem(lat + off, lat_n)
        copy = remote(
            snd2.at[peer], recv2.at[lat], s2.at[off - 1], r2.at[off - 1], (peer, lon)
        )
        copy.start()
        second.append(copy)
    recv2[lat] = snd2[lat]
    quad_weight = (math.pi / nlat) * jnp.sin(
        (lax.broadcasted_iota(jnp.int32, (1, nlat), 1).astype(jnp.float32) + 0.5) * math.pi / nlat
    )
    tables = [legendre[:, t, :] for t in range(count)]
    for copy in second:
        copy.wait()

    for t in range(count):
        cells = recv2[:, t * rows : (t + 1) * rows, :].astype(jnp.float32)
        cells = cells.reshape(lat_n * rows, chans).astype(jnp.bfloat16)
        analysis = (tables[t] * quad_weight).astype(jnp.bfloat16)
        spectra = jnp.dot(analysis, cells, preferred_element_type=jnp.float32)
        filtered = (spectra * filt_ref[...]).astype(jnp.bfloat16)
        result = jnp.dot(
            tables[t].T.astype(jnp.bfloat16), filtered, preferred_element_type=jnp.float32
        )
        back[:, t * rows : (t + 1) * rows, :] = result.reshape(lat_n, rows, chans)
    for d in range(lat_n):
        snd3[d] = back[d].astype(wire)

    third = []
    for off in range(1, lat_n):
        peer = lax.rem(lat + off, lat_n)
        copy = remote(
            snd3.at[peer], out_ref.at[place, lat], s3.at[off - 1], r3.at[off - 1], (peer, lon)
        )
        copy.start()
        third.append(copy)
    out_ref[place, lat] = snd3[lat]

    last = []

    def spread(slot):
        source = lax.rem(lat + lat_n - slot, lat_n)
        block = out_ref.at[place, source]
        hops = []
        for off in range(1, chips):
            peer = lax.rem(chip + off, chips)
            hops.append(
                remote(
                    block, block, sx.at[slot, off - 1], rx.at[slot, off - 1],
                    (lat, peer * 2 + core),
                )
            )
            hops[-1].start()
        last.append(remote(block, block, sp.at[slot], rp.at[slot], (lat, mate)))
        last[-1].start()
        return hops

    def forward_on(slot, hops):
        source = lax.rem(lat + lat_n - slot, lat_n)
        for off in range(1, chips):
            hops[off - 1].wait()
            origin = core * chips + lax.rem(chip + chips - off, chips)
            block = out_ref.at[origin, source]
            last.append(
                remote(block, block, sf.at[slot, off - 1], rf.at[slot, off - 1], (lat, mate))
            )
            last[-1].start()

    hops = {}
    for slot in range(lat_n):
        if slot:
            third[slot - 1].wait()
        hops[slot] = spread(slot)
        if slot >= 3:
            forward_on(slot - 3, hops[slot - 3])
    for slot in range(max(lat_n - 3, 0), lat_n):
        forward_on(slot, hops[slot])
    for copy in last:
        copy.wait()
    for row in range(rows):
        put(row).wait()


def output_kernel(syn_ref, ac_ref, table_ref, mix_ref, o_ref, wide):
    rows, width, chans = ac_ref.shape
    all_q = table_ref.shape[1]
    wide[...] = syn_ref[...].astype(jnp.float32).reshape(all_q, rows, chans)
    for row in range(rows):
        waves = wide[:, row, :].astype(jnp.bfloat16)
        field = jnp.dot(table_ref[...], waves, preferred_element_type=jnp.float32)
        active = jax.nn.gelu(field, approximate=True).astype(jnp.bfloat16)
        total = ac_ref[row] + jnp.dot(active, mix_ref[...], preferred_element_type=jnp.float32)
        o_ref[:, row, :] = total.T


def per_device(
    grid_field,
    disco_dlat,
    disco_dlon,
    disco_basis,
    disco_quad,
    disco_weight,
    norm_gain,
    spectral_filter,
    mix_weight,
):
    lat_n = lax.axis_size("lat")
    lon_n = lax.axis_size("lon")
    chans, rows, width = grid_field.shape
    nlat, nlon = rows * lat_n, width * lon_n
    modes = M_DEV * lat_n
    all_q = 2 * modes
    degrees = spectral_filter.shape[1]
    group = all_q // lon_n
    count = group // lat_n
    basis_count = disco_weight.shape[0]
    f32, bf16 = jnp.float32, jnp.bfloat16

    wire = bf16 if (count * rows) % 16 == 0 else f32
    block = (lat_n, count * rows, chans)
    chips = lon_n // 2
    tall = width + 2 * PAD
    dma = pltpu.SemaphoreType.DMA
    vmem = pltpu.VMEM
    synthesis, after_conv, inverse = pl.pallas_call(
        functools.partial(field_kernel, lat_n, lon_n, modes),
        out_shape=(
            jax.ShapeDtypeStruct((lon_n,) + block, wire),
            jax.ShapeDtypeStruct((rows, width, chans), f32),
            jax.ShapeDtypeStruct((width, all_q), bf16),
        ),
        in_specs=[SM] * 4 + [HB, HB, VM, VM],
        out_specs=(VM, HB, VM),
        scratch_shapes=[
            vmem((chans, rows, width), f32),
            vmem(disco_weight.shape, bf16),
            vmem((rows, width, chans), f32),
            dma((chans // LANES,)), dma, dma((rows,)),
            vmem((rows + 2 * HALO, tall, chans), bf16),
            vmem(
                ((basis_count + 1) // 2, rows + 2 * HALO, chans // LANES, 2 * tall, LANES), f32
            ),
            vmem((all_q, width), bf16),
            vmem((rows, 2, all_q // 2, chans), bf16),
            vmem((rows, all_q // 2, chans), bf16),
            vmem((rows, chips, group, chans), bf16),
            vmem((chips - 1, rows, group, chans), bf16),
            vmem((group, rows, chans), f32),
            vmem(block, wire),
            vmem(block, wire),
            vmem((degrees, count, nlat), f32),
            vmem((2, count, nlat), f32),
            vmem(block, f32),
            vmem(block, wire),
            dma((9,)), dma((9,)),
            dma((rows,)), dma((rows,)),
            dma((rows, chips - 1)), dma((rows, chips - 1)),
            dma((lat_n - 1,)), dma((lat_n - 1,)),
            dma((lat_n - 1,)), dma((lat_n - 1,)),
            dma((lat_n, chips - 1)), dma((lat_n, chips - 1)),
            dma((lat_n,)), dma((lat_n,)),
            dma((lat_n, chips - 1)), dma((lat_n, chips - 1)),
        ],
        compiler_params=pltpu.CompilerParams(collective_id=0, has_side_effects=True),
    )(
        disco_dlat, disco_dlon, disco_basis, disco_quad,
        grid_field, disco_weight, norm_gain, spectral_filter.T,
    )

    return pl.pallas_call(
        output_kernel,
        out_shape=jax.ShapeDtypeStruct((chans, rows, width), f32),
        in_specs=[VM] * 4,
        out_specs=VM,
        scratch_shapes=[pltpu.VMEM((all_q, rows, chans), f32)],
    )(synthesis, after_conv, inverse, mix_weight)


def solution(mesh):
    placed = (
        P(None, "lat", "lon"),
        P("lat", None),
        P("lat", None),
        P("lat", None),
        P("lat", None),
        P(),
        P(),
        P(),
        P(),
    )
    return jax.shard_map(
        per_device, mesh=mesh, in_specs=placed, out_specs=P(None, "lat", "lon"), check_vma=False
    )
```
